32 devices in a mesh: tm: 16 (over z, y, x), tensor: 2 (over core).
Axes of the slice: x: 2, y: 2, z: 4, core: 2. Of those that a mesh axis runs over, the one named last changes fastest.
Arguments:
- frames: bfloat16 [32768, 1024], P('tm'), may hold values from -6 to 6
- utt_ids: int32 [32768], P('tm'), may hold values from 0 to 63, never falling along the last dimension, each value on 1 to 1024 neighbouring positions
- seg_ids: int32 [32768], P('tm'), may hold values from 0 to 1023, as said below
- norm_gain: float32 [1024], replicated, may hold values from 0.1 to 1.9
- w_value: bfloat16 [1024, 1024], P(None, 'tensor'), may hold values from -0.1875 to 0.1875
- w_gate: bfloat16 [1024, 1024], P(None, 'tensor'), may hold values from -0.1875 to 0.1875
- conv_taps: float32 [31, 1024], P(None, 'tensor'), may hold values from -2 to 2
- bn_scale: float32 [1024], P('tensor'), may hold values from 0.1 to 1.9
- bn_shift: float32 [1024], P('tensor'), may hold values from -3 to 3
- w_out: bfloat16 [1024, 1024], P('tensor'), may hold values from -0.375 to 0.375
Outputs:
- compressed: float32 [1024, 1024], P('tm', 'tensor')
The draws below stay inside these ranges and needn't reach their ends.
Inputs may be any that keep to these rules, and one draw needn't show every extreme that they name: `seg_ids`: never falling; segment s is owned by index s // 64 of tm, each owner has 64 segments of one or more frames; the frames of index i of tm name only segments owned by indices i and i + 1, the latter only in its last 256 frames. `utt_ids`: never falling; each utterance has 1 to 1024 frames.
All inputs are finite; a program needn't handle non-finite values.
Results may differ from the reference program's by a relative error of at most 0.008.
Values may be sent and summed in bfloat16 or wider, within the bound.
A program may use at most 64 MiB of HBM per device.

```python
import math
import jax
import jax.numpy as jnp
import numpy as np
from jax import lax

D = 1024
KERNEL = 31
F_DEV = 2048
UTT_MOST = 1024
SEG_DEV = 64
FRAMES = 32768
SEGS = 1024
UTTS = 64


def draw_seg_ids(key, part):
    devices = FRAMES // F_DEV
    key_shift, key_weight = jax.random.split(jax.random.fold_in(key, 17))
    reach = F_DEV // 8
    moves = jax.random.randint(key_shift, (devices,), -reach, 1).astype(jnp.int32)
    moves = moves.at[0].set(0)
    moves = moves.at[devices - 1].set(-reach)
    starts = jnp.arange(devices, dtype=jnp.int32) * F_DEV + moves
    ends = jnp.concatenate([starts[1:], jnp.full((1,), FRAMES, jnp.int32)])
    spans = ends - starts
    weights = jax.random.randint(key_weight, (devices, SEG_DEV), 6, 9).astype(jnp.int32)
    totals = jnp.cumsum(weights, axis=1)
    bounds = jnp.arange(1, SEG_DEV + 1, dtype=jnp.int32)[None, :] + (spans[:, None] - SEG_DEV) * totals // totals[:, -1:]
    position = jnp.arange(FRAMES, dtype=jnp.int32)
    owner = jnp.sum((starts[None, :] <= position[:, None]).astype(jnp.int32), axis=1) - 1
    offset = position - starts[owner]
    local = jnp.sum((bounds[owner] <= offset[:, None]).astype(jnp.int32), axis=1)
    return (owner * SEG_DEV + local).astype(jnp.int32)


def steps_of(own_key, dims, pieces, smallest, top_value):
    def one(axis_at, blocks):
        draws = jax.random.uniform(jax.random.fold_in(jax.random.fold_in(own_key, 6), axis_at), (blocks,), jnp.float32, smallest / len(pieces), top_value / len(pieces))
        return jnp.repeat(jnp.exp(draws), dims[axis_at] // blocks).reshape((-1,) + (1,) * (len(dims) - axis_at - 1))

    level = one(*pieces[0])
    for cut in pieces[1:]:
        level = level * one(*cut)
    return level


def length_profile(amount, total, most, slope):
    loads = [(1 << 20) // math.isqrt(grade ** slope) + 1 for grade in range(2, amount + 1)]
    spare, given = total - most - (amount - 1), [1] * (amount - 1)
    while spare > 0:
        free = [i for i in range(amount - 1) if given[i] < most]
        pool, budget = sum([loads[i] for i in free]), spare
        for i in free:
            extra = min(most - given[i], max(1, budget * loads[i] // pool), spare)
            given[i] = given[i] + extra
            spare = spare - extra
    return np.array([most] + given)


def uneven_parts(key, amount, total, most, lean):
    if amount == 2:
        one = jax.random.randint(key, (), max(1, total - most), min(most, total - 1) + 1)
        return jnp.stack([one, total - one])
    lengths = jnp.asarray(length_profile(amount, total, most, lean), jnp.int32)
    pairs = (amount - 1) // 2
    giver, receiver = lengths[1:1 + 2 * pairs:2], lengths[2:2 + 2 * pairs:2]
    margin = jnp.minimum(giver - 1, most - receiver)
    moved = jax.random.randint(jax.random.fold_in(key, 1), (pairs,), 0, 1 << 20) % (margin + 1)
    lengths = lengths.at[1:1 + 2 * pairs:2].set(giver - moved).at[2:2 + 2 * pairs:2].set(receiver + moved)
    return lengths[jax.random.permutation(jax.random.fold_in(key, 2), amount)]


def gaussian(own_key, shape, scale, most, shards=(), kind=jnp.bfloat16):
    result = scale * jax.random.normal(own_key, shape, jnp.float32)
    if shards:
        result = result * steps_of(own_key, shape, shards, -0.22, 0.18)
    return jnp.clip(result, -most, most).astype(kind)


def setup_inputs(seed: int = 0) -> dict:
    keys = jax.random.split(jax.random.key(seed), 11)
    frames = gaussian(keys[0], (FRAMES, D), 1.0, 6.0, ((0, 16),))
    utt_ids = jnp.searchsorted(jnp.cumsum(uneven_parts(keys[1], UTTS, FRAMES, UTT_MOST, 2)), jnp.arange(FRAMES), side="right").astype(jnp.int32)
    seg_ids = draw_seg_ids(jax.random.fold_in(keys[10], 71), 0)
    norm_gain = jnp.clip(1.0 + 0.18 * jax.random.normal(keys[3], (D,), jnp.float32), 0.1, 1.9)
    w_value = gaussian(keys[4], (D, D), D ** -0.5, 0.1875, ((1, 2),))
    w_gate = gaussian(keys[5], (D, D), D ** -0.5, 0.1875, ((1, 2),))
    conv_taps = gaussian(keys[6], (KERNEL, D), 8 ** -0.5, 2.0, ((1, 2),), jnp.float32)
    bn_scale = jnp.clip(1.0 + 0.18 * jax.random.normal(keys[7], (D,), jnp.float32), 0.1, 1.9)
    bn_shift = gaussian(keys[8], (D,), 0.5, 3.0, ((0, 2),), jnp.float32)
    w_out = gaussian(keys[9], (D, D), (D // 4) ** -0.5, 0.375, ((0, 2),))
    return {"frames": frames, "utt_ids": utt_ids, "seg_ids": seg_ids, "norm_gain": norm_gain, "w_value": w_value, "w_gate": w_gate, "conv_taps": conv_taps, "bn_scale": bn_scale, "bn_shift": bn_shift, "w_out": w_out}


def reference(frames, utt_ids, seg_ids, norm_gain, w_value, w_gate, conv_taps, bn_scale, bn_shift, w_out):
    floats = frames.astype(jnp.float32)
    center = lax.optimization_barrier(jnp.mean(floats, axis=1, keepdims=True))
    spread = lax.optimization_barrier(jnp.mean((floats - center) ** 2, axis=1, keepdims=True))
    normed = ((floats - center) * lax.rsqrt(spread + 1e-05) * norm_gain).astype(jnp.bfloat16)
    value = jnp.dot(normed, w_value, preferred_element_type=jnp.float32)
    gate = jnp.dot(normed, w_gate, preferred_element_type=jnp.float32)
    glu = (value * jax.nn.sigmoid(gate)).astype(jnp.bfloat16)
    half = (KERNEL - 1) // 2
    padded = jnp.pad(glu, ((half, half), (0, 0)))
    labels = jnp.pad(utt_ids, (half, half), constant_values=-1)
    conv = jnp.zeros(glu.shape, jnp.float32)
    for tap in range(KERNEL):
        same = (labels[tap:tap + FRAMES] == utt_ids).astype(jnp.float32)
        conv = conv + conv_taps[tap] * (padded[tap:tap + FRAMES].astype(jnp.float32) * same[:, None])
    hidden = jax.nn.silu(conv * bn_scale + bn_shift).astype(jnp.bfloat16)
    sum_hidden = jax.ops.segment_sum(hidden.astype(jnp.float32), seg_ids, num_segments=SEGS)
    sum_frames = jax.ops.segment_sum(floats, seg_ids, num_segments=SEGS)
    count = jax.ops.segment_sum(jnp.ones((FRAMES,), jnp.float32), seg_ids, num_segments=SEGS)
    mean_hidden = (sum_hidden / count[:, None]).astype(jnp.bfloat16)
    return sum_frames / count[:, None] + jnp.dot(mean_hidden, w_out, preferred_element_type=jnp.float32)
```

```python
import functools

import jax
import jax.numpy as jnp
from jax import lax
from jax.experimental import pallas as pl
from jax.experimental.pallas import tpu as pltpu
from jax.sharding import PartitionSpec as P

MESH = pl.DeviceIdType.MESH
VMEM = pl.BlockSpec(memory_space=pltpu.VMEM)
HBM = pl.BlockSpec(memory_space=pltpu.HBM)
EDGE = 16
LANES = 128
CHUNK = 256
SUB = 64
MIB = 1 << 20


def sigmoid(v):
    return 0.5 + 0.5 * jnp.tanh(0.5 * v)


def normalised(block, gain):
    floats = block.astype(jnp.float32)
    center = jnp.mean(floats, axis=1, keepdims=True)
    moved = floats - center
    spread = jnp.mean(moved * moved, axis=1, keepdims=True)
    return (moved * lax.rsqrt(spread + 1e-05) * gain).astype(jnp.bfloat16)


def selection(slots, slot_count):
    kinds = lax.broadcasted_iota(jnp.int32, (slot_count, LANES), 0)
    rows = [
        jnp.where(kinds == slots[r : r + 1, :], 1.0, 0.0).astype(jnp.bfloat16)
        for r in range(slots.shape[0])
    ]
    return jnp.concatenate(rows, axis=1)


def glu_kernel(
    tm_count, frames, labels, segs, gain, wv_hbm, wg_hbm,
    glu_out, lab_out, pooled_out,
    held, normed, halo, lab_low, lab_high, wv, wg, chunk_sems, w_sems, send, recv,
):
    rows = frames.shape[0]
    channels = wv.shape[1]
    chunks = rows // CHUNK
    lab_rows = labels.shape[0]
    owned = rows // 32
    me = lax.axis_index("tm")
    column = lax.axis_index("tensor")
    loads = [
        pltpu.make_async_copy(
            frames.at[pl.ds(k * CHUNK, CHUNK)], held.at[pl.ds(k * CHUNK, CHUNK)], chunk_sems.at[k]
        )
        for k in range(chunks)
    ]
    weights = [
        pltpu.make_async_copy(wv_hbm, wv, w_sems.at[0]),
        pltpu.make_async_copy(wg_hbm, wg, w_sems.at[1]),
    ]
    loads[0].start()
    for copy in weights + loads[1:]:
        copy.start()
    up = {"tm": me + 1}
    down = {"tm": me - 1}
    ups = [
        pltpu.make_async_remote_copy(
            frames.at[pl.ds(rows - EDGE, EDGE)], halo.at[pl.ds(0, EDGE)],
            send.at[0], recv.at[0], device_id=up, device_id_type=MESH,
        ),
        pltpu.make_async_remote_copy(
            labels.at[pl.ds(lab_rows - 8, 8)], lab_low,
            send.at[1], recv.at[1], device_id=up, device_id_type=MESH,
        ),
    ]
    downs = [
        pltpu.make_async_remote_copy(
            frames.at[pl.ds(0, EDGE)], halo.at[pl.ds(EDGE, EDGE)],
            send.at[2], recv.at[2], device_id=down, device_id_type=MESH,
        ),
        pltpu.make_async_remote_copy(
            labels.at[pl.ds(0, 8)], lab_high,
            send.at[3], recv.at[3], device_id=down, device_id_type=MESH,
        ),
    ]
    has_low = me > 0
    has_high = me < tm_count - 1
    barrier = pltpu.get_barrier_semaphore()

    @pl.when(has_low)
    def _():
        pl.semaphore_signal(barrier, inc=1, device_id=down, device_id_type=MESH)

    @pl.when(has_high)
    def _():
        pl.semaphore_signal(barrier, inc=1, device_id=up, device_id_type=MESH)

    inner = jnp.logical_and(has_low, has_high)

    @pl.when(inner)
    def _():
        pl.semaphore_wait(barrier, 2)

    @pl.when(jnp.logical_not(inner))
    def _():
        pl.semaphore_wait(barrier, 1)

    @pl.when(has_high)
    def _():
        for copy in ups:
            copy.start()

    @pl.when(has_low)
    def _():
        for copy in downs:
            copy.start()

    @pl.when(jnp.logical_not(has_low))
    def _():
        halo[pl.ds(0, EDGE), :] = jnp.zeros((EDGE, halo.shape[1]), halo.dtype)
        lab_low[...] = jnp.full(lab_low.shape, -1, jnp.int32)

    @pl.when(jnp.logical_not(has_high))
    def _():
        halo[pl.ds(EDGE, EDGE), :] = jnp.zeros((EDGE, halo.shape[1]), halo.dtype)
        lab_high[...] = jnp.full(lab_high.shape, -1, jnp.int32)

    scale = gain[...]
    columns = pl.ds(pl.multiple_of(column * channels, LANES), channels)
    per = CHUNK // LANES
    pooled = jnp.zeros((2 * owned, channels), jnp.float32)

    def prepare(k):
        loads[k].wait()
        normed[k % 2, pl.ds(0, CHUNK), :] = normalised(held[pl.ds(k * CHUNK, CHUNK), :], scale)

    prepare(0)
    for copy in weights:
        copy.wait()
    for k in range(chunks):
        if k + 1 < chunks:
            prepare(k + 1)
        size = CHUNK
        if k == chunks - 1:
            size = CHUNK + 2 * EDGE

            @pl.when(has_low)
            def _():
                ups[0].wait_recv()
                ups[1].wait_recv()

            @pl.when(has_high)
            def _():
                downs[0].wait_recv()
                downs[1].wait_recv()

            normed[k % 2, pl.ds(CHUNK, 2 * EDGE), :] = normalised(halo[...], scale)
        block = normed[k % 2, pl.ds(0, size), :]
        value = jnp.dot(block, wv[...], preferred_element_type=jnp.float32)
        gate = jnp.dot(block, wg[...], preferred_element_type=jnp.float32)
        glu = (value * sigmoid(gate)).astype(jnp.bfloat16)
        glu_out[pl.ds(EDGE + k * CHUNK, CHUNK), :] = glu[:CHUNK]
        if k == chunks - 1:
            glu_out[pl.ds(0, EDGE), :] = glu[CHUNK : CHUNK + EDGE]
            glu_out[pl.ds(EDGE + rows, EDGE), :] = glu[CHUNK + EDGE :]
        slots = segs[pl.ds(k * per, per), :] - me * owned
        pooled = pooled + jnp.dot(
            selection(slots, 2 * owned),
            held[pl.ds(k * CHUNK, CHUNK), columns],
            preferred_element_type=jnp.float32,
        )
    pooled_out[...] = pooled
    lab_out[pl.ds(0, 8), :] = lab_low[...]
    lab_out[pl.ds(8, lab_rows), :] = labels[...]
    lab_out[pl.ds(8 + lab_rows, 8), :] = lab_high[...]

    @pl.when(has_high)
    def _():
        for copy in ups:
            copy.wait_send()

    @pl.when(has_low)
    def _():
        for copy in downs:
            copy.wait_send()


def conv_kernel(
    glu, lab_s, lab_v, segs, taps, bn_scale, bn_shift, pooled_frames, w_hbm,
    message, count_message, own, count_out,
    wide, hidden, lab_wide, w_out, mixed, w_sem,
):
    channels = glu.shape[1]
    rows = hidden.shape[0]
    groups = channels // LANES
    kernel = taps.shape[0]
    half = (kernel - 1) // 2
    owned = rows // 32
    me = lax.axis_index("tm")
    column = lax.axis_index("tensor")
    load = pltpu.make_async_copy(w_hbm, w_out, w_sem)
    load.start()

    def widen(start, size):
        block = glu[pl.ds(start, size), :].astype(jnp.float32)
        for g in range(groups):
            wide[g, pl.ds(start, size), :] = block[:, g * LANES : (g + 1) * LANES]

    widen(0, 2 * EDGE)

    def finish(acc, start, g, size):
        lanes = slice(g * LANES, (g + 1) * LANES)
        v = acc * bn_scale[:, lanes] + bn_shift[:, lanes]
        hidden[pl.ds(start, size), lanes] = (v * sigmoid(v)).astype(jnp.bfloat16)

    def step(i, carry):
        base = pl.multiple_of(i * LANES, LANES)
        widen(pl.multiple_of(base + 2 * EDGE, 2 * EDGE), LANES)

        def label(at):
            return lab_s[7 + i + (LANES + at) // LANES, (LANES + at) % LANES]

        @pl.when(label(-half) != label(LANES - 1 + half))
        def _():
            for d in range(3):
                row = lab_v[pl.ds(7 + i + d, 1), :]
                lab_wide[pl.ds(d * LANES, LANES), :] = jnp.transpose(
                    jnp.broadcast_to(row, (LANES, LANES))
                )

        for o in range(0, LANES, SUB):
            same = label(o - half) == label(o + SUB - 1 + half)

            @pl.when(same)
            def _(o=o):
                for g in range(groups):
                    lanes = slice(g * LANES, (g + 1) * LANES)
                    acc = jnp.zeros((SUB, LANES), jnp.float32)
                    for t in range(kernel):
                        x = wide[g, pl.ds(base + (o + t + EDGE - half), SUB), :]
                        acc = acc + taps[t : t + 1, lanes] * x
                    finish(acc, base + o, g, SUB)

            @pl.when(jnp.logical_not(same))
            def _(o=o):
                for p in range(o, o + SUB, 32):
                    center = lab_wide[pl.ds(LANES + p, 32), :]
                    accs = [jnp.zeros((32, LANES), jnp.float32) for _ in range(groups)]
                    for t in range(kernel):
                        keep = lab_wide[pl.ds(LANES + p + t - half, 32), :] == center
                        for g in range(groups):
                            lanes = slice(g * LANES, (g + 1) * LANES)
                            x = wide[g, pl.ds(base + (p + t + EDGE - half), 32), :]
                            accs[g] = accs[g] + taps[t : t + 1, lanes] * jnp.where(keep, x, 0.0)
                    for g in range(groups):
                        finish(accs[g], base + p, g, 32)

        return carry

    lax.fori_loop(0, rows // LANES, step, 0)

    per = CHUNK // LANES
    total = jnp.zeros((2 * owned, channels), jnp.float32)
    tally = jnp.zeros((2 * owned, LANES), jnp.float32)
    for k in range(rows // CHUNK):
        chosen = selection(segs[pl.ds(k * per, per), :] - me * owned, 2 * owned)
        total = total + jnp.dot(
            chosen, hidden[pl.ds(k * CHUNK, CHUNK), :], preferred_element_type=jnp.float32
        )
        wide_chosen = chosen.astype(jnp.float32)
        for q in range(per):
            tally = tally + wide_chosen[:, q * LANES : (q + 1) * LANES]
    count = jnp.broadcast_to(jnp.sum(tally, axis=1, keepdims=True), tally.shape)
    load.wait()
    high = total.astype(jnp.bfloat16)
    low = (total - high.astype(jnp.float32)).astype(jnp.bfloat16)
    mixed[...] = jnp.dot(high, w_out[...], preferred_element_type=jnp.float32) + jnp.dot(
        low, w_out[...], preferred_element_type=jnp.float32
    )
    for j in range(message.shape[1]):
        lanes = slice(j * channels, (j + 1) * channels)
        message[0, j] = mixed[:owned, lanes].astype(jnp.bfloat16)
        message[1, j] = mixed[owned:, lanes].astype(jnp.bfloat16)
    columns = pl.ds(pl.multiple_of(column * channels, LANES), channels)
    mine = mixed[:, columns] + pooled_frames[...]
    own[...] = mine[:owned]
    message[1, column] = mine[owned:].astype(jnp.bfloat16)
    count_out[...] = count[:owned]
    count_message[...] = count[owned:].astype(jnp.bfloat16)


def exchange_kernel(
    tm_count, n, message, count_message, own, count_own, out,
    from_peer, from_behind, from_count, send, recv,
):
    me = lax.axis_index("tm")
    column = lax.axis_index("tensor")
    has_low = me > 0
    has_high = me < tm_count - 1
    others = [lax.rem(column + s, n) for s in range(n)]
    barrier = pltpu.get_barrier_semaphore()
    for s in range(1, n):
        pl.semaphore_signal(
            barrier, inc=1, device_id={"tensor": others[s]}, device_id_type=MESH
        )

    @pl.when(has_low)
    def _():
        for s in range(n):
            pl.semaphore_signal(
                barrier, inc=1, device_id=(me - 1, others[s]), device_id_type=MESH
            )

    @pl.when(has_high)
    def _():
        pl.semaphore_wait(barrier, 2 * n - 1)

    @pl.when(jnp.logical_not(has_high))
    def _():
        pl.semaphore_wait(barrier, n - 1)

    ahead = [
        pltpu.make_async_remote_copy(
            message.at[1, others[s]], from_behind.at[s], send.at[s], recv.at[s],
            device_id=(me + 1, others[s]), device_id_type=MESH,
        )
        for s in range(n)
    ] + [
        pltpu.make_async_remote_copy(
            count_message, from_count, send.at[n], recv.at[n],
            device_id=(me + 1, column), device_id_type=MESH,
        )
    ]
    across = [
        pltpu.make_async_remote_copy(
            message.at[0, others[s]], from_peer.at[s], send.at[n + s], recv.at[n + s],
            device_id=(me, others[s]), device_id_type=MESH,
        )
        for s in range(1, n)
    ]

    @pl.when(has_high)
    def _():
        for copy in ahead:
            copy.start()

    for copy in across:
        copy.start()

    @pl.when(jnp.logical_not(has_low))
    def _():
        from_behind[...] = jnp.zeros(from_behind.shape, from_behind.dtype)
        from_count[...] = jnp.zeros(from_count.shape, from_count.dtype)

    for copy in across:
        copy.wait_recv()

    @pl.when(has_low)
    def _():
        for copy in ahead:
            copy.wait_recv()

    total = own[...]
    for s in range(1, n):
        total = total + from_peer[s].astype(jnp.float32)
    for s in range(n):
        total = total + from_behind[s].astype(jnp.float32)
    count = count_own[...] + from_count[...].astype(jnp.float32)
    for g in range(out.shape[1] // LANES):
        lanes = slice(g * LANES, (g + 1) * LANES)
        out[:, lanes] = total[:, lanes] / count
    for copy in across:
        copy.wait_send()

    @pl.when(has_high)
    def _():
        for copy in ahead:
            copy.wait_send()


def shards(
    tm_count, n,
    frames, utt_ids, seg_ids, norm_gain, w_value, w_gate, conv_taps, bn_scale, bn_shift, w_out
):
    rows, width = frames.shape
    channels = w_value.shape[1]
    owned = rows // 32
    lab_rows = rows // LANES
    bf16, f32, i32 = jnp.bfloat16, jnp.float32, jnp.int32
    shape = jax.ShapeDtypeStruct
    dma = pltpu.SemaphoreType.DMA
    labels = utt_ids.reshape(lab_rows, LANES)
    segs = seg_ids.reshape(lab_rows, LANES)
    glu, lab, pooled = pl.pallas_call(
        functools.partial(glu_kernel, tm_count),
        name="glu",
        out_shape=[
            shape((rows + 2 * EDGE, channels), bf16),
            shape((lab_rows + 16, LANES), i32),
            shape((2 * owned, channels), f32),
        ],
        in_specs=[HBM, VMEM, VMEM, VMEM, HBM, HBM],
        out_specs=[VMEM, VMEM, VMEM],
        scratch_shapes=[
            pltpu.VMEM((rows, width), bf16),
            pltpu.VMEM((2, CHUNK + 2 * EDGE, width), bf16),
            pltpu.VMEM((2 * EDGE, width), bf16),
            pltpu.VMEM((8, LANES), i32),
            pltpu.VMEM((8, LANES), i32),
            pltpu.VMEM((width, channels), bf16),
            pltpu.VMEM((width, channels), bf16),
            dma((rows // CHUNK,)),
            dma((2,)),
            dma((4,)),
            dma((4,)),
        ],
        compiler_params=pltpu.CompilerParams(
            collective_id=0, has_side_effects=True, vmem_limit_bytes=61 * MIB
        ),
    )(frames, labels, segs, norm_gain.reshape(1, width), w_value, w_gate)
    message, count_message, own, count = pl.pallas_call(
        conv_kernel,
        name="conv",
        out_shape=[
            shape((2, n, owned, channels), bf16),
            shape((owned, LANES), bf16),
            shape((owned, channels), f32),
            shape((owned, LANES), f32),
        ],
        in_specs=[VMEM, pl.BlockSpec(memory_space=pltpu.SMEM)] + [VMEM] * 6 + [HBM],
        out_specs=[VMEM] * 4,
        scratch_shapes=[
            pltpu.VMEM((channels // LANES, rows + 2 * EDGE, LANES), f32),
            pltpu.VMEM((rows, channels), bf16),
            pltpu.VMEM((3 * LANES, LANES), i32),
            pltpu.VMEM(w_out.shape, bf16),
            pltpu.VMEM((2 * owned, w_out.shape[1]), f32),
            dma(()),
        ],
        compiler_params=pltpu.CompilerParams(vmem_limit_bytes=32 * MIB),
    )(
        glu, lab, lab, segs, conv_taps, bn_scale.reshape(1, channels),
        bn_shift.reshape(1, channels), pooled, w_out,
    )
    return pl.pallas_call(
        functools.partial(exchange_kernel, tm_count, n),
        name="exchange",
        out_shape=shape((owned, channels), f32),
        in_specs=[VMEM] * 4,
        out_specs=VMEM,
        scratch_shapes=[
            pltpu.VMEM((n, owned, channels), bf16),
            pltpu.VMEM((n, owned, channels), bf16),
            pltpu.VMEM((owned, LANES), bf16),
            dma((2 * n,)),
            dma((2 * n,)),
        ],
        compiler_params=pltpu.CompilerParams(
            collective_id=1, has_side_effects=True, vmem_limit_bytes=8 * MIB
        ),
    )(message, count_message, own, count)


def solution(mesh):
    in_specs = (
        P("tm", None),
        P("tm"),
        P("tm"),
        P(),
        P(None, "tensor"),
        P(None, "tensor"),
        P(None, "tensor"),
        P("tensor"),
        P("tensor"),
        P("tensor", None),
    )
    out_specs = P("tm", "tensor")
    body = functools.partial(shards, mesh.shape["tm"], mesh.shape["tensor"])
    return jax.shard_map(body, mesh=mesh, in_specs=in_specs, out_specs=out_specs, check_vma=False)
```

```python
import functools

import jax
import jax.numpy as jnp
from jax import lax
from jax.experimental import pallas as pl
from jax.experimental.pallas import tpu as pltpu
from jax.sharding import PartitionSpec as P

MESH = pl.DeviceIdType.MESH
VMEM = pl.BlockSpec(memory_space=pltpu.VMEM)
HBM = pl.BlockSpec(memory_space=pltpu.HBM)
EDGE = 16
LANES = 128
CHUNK = 256
SUB = 64
MIB = 1 << 20


def sigmoid(v):
    return 0.5 + 0.5 * jnp.tanh(0.5 * v)


def normalised(block, gain):
    floats = block.astype(jnp.float32)
    center = jnp.mean(floats, axis=1, keepdims=True)
    moved = floats - center
    spread = jnp.mean(moved * moved, axis=1, keepdims=True)
    return (moved * lax.rsqrt(spread + 1e-05) * gain).astype(jnp.bfloat16)


def selection(slots, slot_count):
    kinds = lax.broadcasted_iota(jnp.int32, (slot_count, LANES), 0)
    rows = [
        jnp.where(kinds == slots[r : r + 1, :], 1.0, 0.0).astype(jnp.bfloat16)
        for r in range(slots.shape[0])
    ]
    return jnp.concatenate(rows, axis=1)


def glu_kernel(
    tm_count, frames, labels, segs, gain, wv_hbm, wg_hbm,
    glu_out, lab_out, pooled_out,
    held, normed, halo, lab_low, lab_high, wv, wg, made, chunk_sems, w_sems, send, recv, out_sems,
):
    rows = frames.shape[0]
    channels = wv.shape[1]
    chunks = rows // CHUNK
    lab_rows = labels.shape[0]
    owned = rows // 32
    me = lax.axis_index("tm")
    column = lax.axis_index("tensor")
    loads = [
        pltpu.make_async_copy(
            frames.at[pl.ds(k * CHUNK, CHUNK)], held.at[pl.ds(k * CHUNK, CHUNK)], chunk_sems.at[k]
        )
        for k in range(chunks)
    ]
    weights = [
        pltpu.make_async_copy(wv_hbm, wv, w_sems.at[0]),
        pltpu.make_async_copy(wg_hbm, wg, w_sems.at[1]),
    ]
    loads[0].start()
    for copy in weights + loads[1:]:
        copy.start()
    up = {"tm": me + 1}
    down = {"tm": me - 1}
    ups = [
        pltpu.make_async_remote_copy(
            frames.at[pl.ds(rows - EDGE, EDGE)], halo.at[pl.ds(0, EDGE)],
            send.at[0], recv.at[0], device_id=up, device_id_type=MESH,
        ),
        pltpu.make_async_remote_copy(
            labels.at[pl.ds(lab_rows - 8, 8)], lab_low,
            send.at[1], recv.at[1], device_id=up, device_id_type=MESH,
        ),
    ]
    downs = [
        pltpu.make_async_remote_copy(
            frames.at[pl.ds(0, EDGE)], halo.at[pl.ds(EDGE, EDGE)],
            send.at[2], recv.at[2], device_id=down, device_id_type=MESH,
        ),
        pltpu.make_async_remote_copy(
            labels.at[pl.ds(0, 8)], lab_high,
            send.at[3], recv.at[3], device_id=down, device_id_type=MESH,
        ),
    ]
    has_low = me > 0
    has_high = me < tm_count - 1
    barrier = pltpu.get_barrier_semaphore()

    @pl.when(has_low)
    def _():
        pl.semaphore_signal(barrier, inc=1, device_id=down, device_id_type=MESH)

    @pl.when(has_high)
    def _():
        pl.semaphore_signal(barrier, inc=1, device_id=up, device_id_type=MESH)

    inner = jnp.logical_and(has_low, has_high)

    @pl.when(inner)
    def _():
        pl.semaphore_wait(barrier, 2)

    @pl.when(jnp.logical_not(inner))
    def _():
        pl.semaphore_wait(barrier, 1)

    @pl.when(has_high)
    def _():
        for copy in ups:
            copy.start()

    @pl.when(has_low)
    def _():
        for copy in downs:
            copy.start()

    @pl.when(jnp.logical_not(has_low))
    def _():
        halo[pl.ds(0, EDGE), :] = jnp.zeros((EDGE, halo.shape[1]), halo.dtype)
        lab_low[...] = jnp.full(lab_low.shape, -1, jnp.int32)

    @pl.when(jnp.logical_not(has_high))
    def _():
        halo[pl.ds(EDGE, EDGE), :] = jnp.zeros((EDGE, halo.shape[1]), halo.dtype)
        lab_high[...] = jnp.full(lab_high.shape, -1, jnp.int32)

    scale = gain[...]
    columns = pl.ds(pl.multiple_of(column * channels, LANES), channels)
    per = CHUNK // LANES
    pooled = jnp.zeros((2 * owned, channels), jnp.float32)

    width = min(channels, 256)
    slices = channels // width
    part = CHUNK // slices

    def prepare(k, j):
        normed[k % 2, pl.ds(j * part, part), :] = normalised(
            held[pl.ds(k * CHUNK + j * part, part), :], scale
        )

    def store(start, size, sem):
        here = pl.ds(start, size)
        return pltpu.make_async_copy(made.at[here], glu_out.at[here], out_sems.at[sem])

    stores = [store(EDGE + k * CHUNK, CHUNK, k) for k in range(chunks - 1)]
    stores.append(store(EDGE + rows - CHUNK, CHUNK + EDGE, chunks - 1))
    stores.append(store(0, EDGE, chunks))

    loads[0].wait()
    for j in range(slices):
        prepare(0, j)
    for copy in weights:
        copy.wait()
    for k in range(chunks):
        size = CHUNK
        if k + 1 < chunks:
            loads[k + 1].wait()
        else:
            size = CHUNK + 2 * EDGE

            @pl.when(has_low)
            def _():
                ups[0].wait_recv()
                ups[1].wait_recv()

            @pl.when(has_high)
            def _():
                downs[0].wait_recv()
                downs[1].wait_recv()

            normed[k % 2, pl.ds(CHUNK, 2 * EDGE), :] = normalised(halo[...], scale)
        block = normed[k % 2, pl.ds(0, size), :]
        for j in range(slices):
            lanes = slice(j * width, (j + 1) * width)
            value = jnp.dot(block, wv[:, lanes], preferred_element_type=jnp.float32)
            gate = jnp.dot(block, wg[:, lanes], preferred_element_type=jnp.float32)
            if k + 1 < chunks:
                prepare(k + 1, j)
            glu = (value * sigmoid(gate)).astype(jnp.bfloat16)
            made[pl.ds(EDGE + k * CHUNK, CHUNK), lanes] = glu[:CHUNK]
            if k == chunks - 1:
                made[pl.ds(0, EDGE), lanes] = glu[CHUNK : CHUNK + EDGE]
                made[pl.ds(EDGE + rows, EDGE), lanes] = glu[CHUNK + EDGE :]
        stores[k].start()
        if k == chunks - 1:
            stores[k + 1].start()
        slots = segs[pl.ds(k * per, per), :] - me * owned
        pooled = pooled + jnp.dot(
            selection(slots, 2 * owned),
            held[pl.ds(k * CHUNK, CHUNK), columns],
            preferred_element_type=jnp.float32,
        )
    pooled_out[...] = pooled
    lab_out[pl.ds(0, 8), :] = lab_low[...]
    lab_out[pl.ds(8, lab_rows), :] = labels[...]
    lab_out[pl.ds(8 + lab_rows, 8), :] = lab_high[...]
    for copy in stores:
        copy.wait()

    @pl.when(has_high)
    def _():
        for copy in ups:
            copy.wait_send()

    @pl.when(has_low)
    def _():
        for copy in downs:
            copy.wait_send()


def conv_kernel(
    glu_hbm, lab_s, lab_v, segs, taps, bn_scale, bn_shift, pooled_hbm, w_hbm,
    message, count_message, own, count_out,
    wide, hidden, lab_wide, w_out, mixed, glu, pooled_frames, sems, glu_sems,
):
    channels = glu.shape[1]
    rows = hidden.shape[0]
    groups = channels // LANES
    kernel = taps.shape[0]
    half = (kernel - 1) // 2
    owned = rows // 32
    me = lax.axis_index("tm")
    column = lax.axis_index("tensor")

    def piece(start, size, k):
        here = pl.ds(start, size)
        return pltpu.make_async_copy(glu_hbm.at[here], glu.at[here], glu_sems.at[k])

    first = piece(0, CHUNK + 2 * EDGE, 0)
    first.start()
    for k in range(1, rows // CHUNK):
        piece(k * CHUNK + 2 * EDGE, CHUNK, k).start()
    late = [
        pltpu.make_async_copy(w_hbm, w_out, sems.at[0]),
        pltpu.make_async_copy(pooled_hbm, pooled_frames, sems.at[1]),
    ]
    for copy in late:
        copy.start()
    first.wait()

    def widen(start, size):
        block = glu[pl.ds(start, size), :].astype(jnp.float32)
        for g in range(groups):
            wide[g, pl.ds(start, size), :] = block[:, g * LANES : (g + 1) * LANES]

    widen(0, 2 * EDGE)

    def finish(acc, start, g, size):
        lanes = slice(g * LANES, (g + 1) * LANES)
        v = acc * bn_scale[:, lanes] + bn_shift[:, lanes]
        hidden[pl.ds(start, size), lanes] = (v * sigmoid(v)).astype(jnp.bfloat16)

    def step(i, carry):
        base = pl.multiple_of(i * LANES, LANES)
        k = i // (CHUNK // LANES)

        @pl.when(jnp.logical_and(i > 0, k * (CHUNK // LANES) == i))
        def _():
            piece(pl.multiple_of(k * CHUNK + 2 * EDGE, 2 * EDGE), CHUNK, k).wait()

        widen(pl.multiple_of(base + 2 * EDGE, 2 * EDGE), LANES)

        def label(at):
            return lab_s[7 + i + (LANES + at) // LANES, (LANES + at) % LANES]

        @pl.when(label(-half) != label(LANES - 1 + half))
        def _():
            for d in range(3):
                row = lab_v[pl.ds(7 + i + d, 1), :]
                lab_wide[pl.ds(d * LANES, LANES), :] = jnp.transpose(
                    jnp.broadcast_to(row, (LANES, LANES))
                )

        for o in range(0, LANES, SUB):
            same = label(o - half) == label(o + SUB - 1 + half)

            @pl.when(same)
            def _(o=o):
                for g in range(groups):
                    lanes = slice(g * LANES, (g + 1) * LANES)
                    acc = jnp.zeros((SUB, LANES), jnp.float32)
                    for t in range(kernel):
                        x = wide[g, pl.ds(base + (o + t + EDGE - half), SUB), :]
                        acc = acc + taps[t : t + 1, lanes] * x
                    finish(acc, base + o, g, SUB)

            @pl.when(jnp.logical_not(same))
            def _(o=o):
                for p in range(o, o + SUB, 32):
                    center = lab_wide[pl.ds(LANES + p, 32), :]
                    accs = [jnp.zeros((32, LANES), jnp.float32) for _ in range(groups)]
                    for t in range(kernel):
                        keep = lab_wide[pl.ds(LANES + p + t - half, 32), :] == center
                        for g in range(groups):
                            lanes = slice(g * LANES, (g + 1) * LANES)
                            x = wide[g, pl.ds(base + (p + t + EDGE - half), 32), :]
                            accs[g] = accs[g] + taps[t : t + 1, lanes] * jnp.where(keep, x, 0.0)
                    for g in range(groups):
                        finish(accs[g], base + p, g, 32)

        return carry

    lax.fori_loop(0, rows // LANES, step, 0)

    per = CHUNK // LANES
    total = jnp.zeros((2 * owned, channels), jnp.float32)
    tally = jnp.zeros((2 * owned, LANES), jnp.float32)
    for k in range(rows // CHUNK):
        chosen = selection(segs[pl.ds(k * per, per), :] - me * owned, 2 * owned)
        total = total + jnp.dot(
            chosen, hidden[pl.ds(k * CHUNK, CHUNK), :], preferred_element_type=jnp.float32
        )
        wide_chosen = chosen.astype(jnp.float32)
        for q in range(per):
            tally = tally + wide_chosen[:, q * LANES : (q + 1) * LANES]
    count = jnp.broadcast_to(jnp.sum(tally, axis=1, keepdims=True), tally.shape)
    for copy in late:
        copy.wait()
    mixed[...] = jnp.dot(
        total.astype(jnp.bfloat16), w_out[...], preferred_element_type=jnp.float32
    )
    for j in range(message.shape[1]):
        lanes = slice(j * channels, (j + 1) * channels)
        message[0, j] = mixed[:owned, lanes].astype(jnp.bfloat16)
        message[1, j] = mixed[owned:, lanes].astype(jnp.bfloat16)
    columns = pl.ds(pl.multiple_of(column * channels, LANES), channels)
    mine = mixed[:, columns] + pooled_frames[...]
    own[...] = mine[:owned]
    message[1, column] = mine[owned:].astype(jnp.bfloat16)
    count_out[...] = count[:owned]
    count_message[...] = count[owned:].astype(jnp.bfloat16)


def exchange_kernel(
    tm_count, n, message, count_message, own, count_own, out,
    from_peer, from_behind, from_count, send, recv,
):
    me = lax.axis_index("tm")
    column = lax.axis_index("tensor")
    has_low = me > 0
    has_high = me < tm_count - 1
    others = [lax.rem(column + s, n) for s in range(n)]
    barrier = pltpu.get_barrier_semaphore()
    for s in range(1, n):
        pl.semaphore_signal(
            barrier, inc=1, device_id={"tensor": others[s]}, device_id_type=MESH
        )

    @pl.when(has_low)
    def _():
        for s in range(n):
            pl.semaphore_signal(
                barrier, inc=1, device_id=(me - 1, others[s]), device_id_type=MESH
            )

    @pl.when(has_high)
    def _():
        pl.semaphore_wait(barrier, 2 * n - 1)

    @pl.when(jnp.logical_not(has_high))
    def _():
        pl.semaphore_wait(barrier, n - 1)

    ahead = [
        pltpu.make_async_remote_copy(
            message.at[1, others[s]], from_behind.at[s], send.at[s], recv.at[s],
            device_id=(me + 1, others[s]), device_id_type=MESH,
        )
        for s in range(n)
    ] + [
        pltpu.make_async_remote_copy(
            count_message, from_count, send.at[n], recv.at[n],
            device_id=(me + 1, column), device_id_type=MESH,
        )
    ]
    across = [
        pltpu.make_async_remote_copy(
            message.at[0, others[s]], from_peer.at[s], send.at[n + s], recv.at[n + s],
            device_id=(me, others[s]), device_id_type=MESH,
        )
        for s in range(1, n)
    ]

    @pl.when(has_high)
    def _():
        for copy in ahead:
            copy.start()

    for copy in across:
        copy.start()

    @pl.when(jnp.logical_not(has_low))
    def _():
        from_behind[...] = jnp.zeros(from_behind.shape, from_behind.dtype)
        from_count[...] = jnp.zeros(from_count.shape, from_count.dtype)

    for copy in across:
        copy.wait_recv()

    @pl.when(has_low)
    def _():
        for copy in ahead:
            copy.wait_recv()

    total = own[...]
    for s in range(1, n):
        total = total + from_peer[s].astype(jnp.float32)
    for s in range(n):
        total = total + from_behind[s].astype(jnp.float32)
    count = count_own[...] + from_count[...].astype(jnp.float32)
    for g in range(out.shape[1] // LANES):
        lanes = slice(g * LANES, (g + 1) * LANES)
        out[:, lanes] = total[:, lanes] / count
    for copy in across:
        copy.wait_send()

    @pl.when(has_high)
    def _():
        for copy in ahead:
            copy.wait_send()


def shards(
    tm_count, n,
    frames, utt_ids, seg_ids, norm_gain, w_value, w_gate, conv_taps, bn_scale, bn_shift, w_out
):
    rows, width = frames.shape
    channels = w_value.shape[1]
    owned = rows // 32
    lab_rows = rows // LANES
    bf16, f32, i32 = jnp.bfloat16, jnp.float32, jnp.int32
    shape = jax.ShapeDtypeStruct
    dma = pltpu.SemaphoreType.DMA
    labels = utt_ids.reshape(lab_rows, LANES)
    segs = seg_ids.reshape(lab_rows, LANES)
    glu, lab, pooled = pl.pallas_call(
        functools.partial(glu_kernel, tm_count),
        name="glu",
        out_shape=[
            shape((rows + 2 * EDGE, channels), bf16),
            shape((lab_rows + 16, LANES), i32),
            shape((2 * owned, channels), f32),
        ],
        in_specs=[HBM, VMEM, VMEM, VMEM, HBM, HBM],
        out_specs=[HBM, VMEM, VMEM],
        scratch_shapes=[
            pltpu.VMEM((rows, width), bf16),
            pltpu.VMEM((2, CHUNK + 2 * EDGE, width), bf16),
            pltpu.VMEM((2 * EDGE, width), bf16),
            pltpu.VMEM((8, LANES), i32),
            pltpu.VMEM((8, LANES), i32),
            pltpu.VMEM((width, channels), bf16),
            pltpu.VMEM((width, channels), bf16),
            pltpu.VMEM((rows + 2 * EDGE, channels), bf16),
            dma((rows // CHUNK,)),
            dma((2,)),
            dma((4,)),
            dma((4,)),
            dma((rows // CHUNK + 1,)),
        ],
        compiler_params=pltpu.CompilerParams(
            collective_id=0, has_side_effects=True, vmem_limit_bytes=60 * MIB
        ),
    )(frames, labels, segs, norm_gain.reshape(1, width), w_value, w_gate)
    message, count_message, own, count = pl.pallas_call(
        conv_kernel,
        name="conv",
        out_shape=[
            shape((2, n, owned, channels), bf16),
            shape((owned, LANES), bf16),
            shape((owned, channels), f32),
            shape((owned, LANES), f32),
        ],
        in_specs=[HBM, pl.BlockSpec(memory_space=pltpu.SMEM)] + [VMEM] * 5 + [HBM, HBM],
        out_specs=[VMEM] * 4,
        scratch_shapes=[
            pltpu.VMEM((channels // LANES, rows + 2 * EDGE, LANES), f32),
            pltpu.VMEM((rows, channels), bf16),
            pltpu.VMEM((3 * LANES, LANES), i32),
            pltpu.VMEM(w_out.shape, bf16),
            pltpu.VMEM((2 * owned, w_out.shape[1]), f32),
            pltpu.VMEM((rows + 2 * EDGE, channels), bf16),
            pltpu.VMEM((2 * owned, channels), f32),
            dma((2,)),
            dma((rows // CHUNK,)),
        ],
        compiler_params=pltpu.CompilerParams(vmem_limit_bytes=60 * MIB),
    )(
        glu, lab, lab, segs, conv_taps, bn_scale.reshape(1, channels),
        bn_shift.reshape(1, channels), pooled, w_out,
    )
    return pl.pallas_call(
        functools.partial(exchange_kernel, tm_count, n),
        name="exchange",
        out_shape=shape((owned, channels), f32),
        in_specs=[HBM] + [VMEM] * 3,
        out_specs=VMEM,
        scratch_shapes=[
            pltpu.VMEM((n, owned, channels), bf16),
            pltpu.VMEM((n, owned, channels), bf16),
            pltpu.VMEM((owned, LANES), bf16),
            dma((2 * n,)),
            dma((2 * n,)),
        ],
        compiler_params=pltpu.CompilerParams(
            collective_id=1, has_side_effects=True, vmem_limit_bytes=60 * MIB
        ),
    )(message, count_message, own, count)


def solution(mesh):
    in_specs = (
        P("tm", None),
        P("tm"),
        P("tm"),
        P(),
        P(None, "tensor"),
        P(None, "tensor"),
        P(None, "tensor"),
        P("tensor"),
        P("tensor"),
        P("tensor", None),
    )
    out_specs = P("tm", "tensor")
    body = functools.partial(shards, mesh.shape["tm"], mesh.shape["tensor"])
    return jax.shard_map(body, mesh=mesh, in_specs=in_specs, out_specs=out_specs, check_vma=False)
```

```python
import functools

import jax
import jax.numpy as jnp
from jax import lax
from jax.experimental import pallas as pl
from jax.experimental.pallas import tpu as pltpu
from jax.sharding import PartitionSpec as P

MESH = pl.DeviceIdType.MESH
VMEM = pl.BlockSpec(memory_space=pltpu.VMEM)
HBM = pl.BlockSpec(memory_space=pltpu.HBM)
EDGE = 16
LANES = 128
CHUNK = 256
SUB = 32
MIB = 1 << 20


def sigmoid(v):
    return 0.5 + 0.5 * jnp.tanh(0.5 * v)


def normalised(block, gain):
    floats = block.astype(jnp.float32)
    center = jnp.mean(floats, axis=1, keepdims=True)
    moved = floats - center
    spread = jnp.mean(moved * moved, axis=1, keepdims=True)
    return (moved * lax.rsqrt(spread + 1e-05) * gain).astype(jnp.bfloat16)


def selection(slots, slot_count):
    kinds = lax.broadcasted_iota(jnp.int32, (slot_count, LANES), 0)
    rows = [
        jnp.where(kinds == slots[r : r + 1, :], 1.0, 0.0).astype(jnp.bfloat16)
        for r in range(slots.shape[0])
    ]
    return jnp.concatenate(rows, axis=1)


def glu_kernel(
    tm_count, frames, labels, segs, gain, wv_hbm, wg_hbm,
    glu_out, lab_out, pooled_out,
    held, normed, halo, lab_low, lab_high, wv, wg, made, chunk_sems, w_sems, send, recv, out_sems,
):
    rows = frames.shape[0]
    channels = wv.shape[1]
    chunks = rows // CHUNK
    lab_rows = labels.shape[0]
    owned = rows // 32
    me = lax.axis_index("tm")
    column = lax.axis_index("tensor")
    loads = [
        pltpu.make_async_copy(
            frames.at[pl.ds(k * CHUNK, CHUNK)], held.at[pl.ds(k * CHUNK, CHUNK)], chunk_sems.at[k]
        )
        for k in range(chunks)
    ]
    weights = [
        pltpu.make_async_copy(wv_hbm, wv, w_sems.at[0]),
        pltpu.make_async_copy(wg_hbm, wg, w_sems.at[1]),
    ]
    loads[0].start()
    for copy in weights + loads[1:]:
        copy.start()
    up = {"tm": me + 1}
    down = {"tm": me - 1}
    ups = [
        pltpu.make_async_remote_copy(
            frames.at[pl.ds(rows - EDGE, EDGE)], halo.at[pl.ds(0, EDGE)],
            send.at[0], recv.at[0], device_id=up, device_id_type=MESH,
        ),
        pltpu.make_async_remote_copy(
            labels.at[pl.ds(lab_rows - 8, 8)], lab_low,
            send.at[1], recv.at[1], device_id=up, device_id_type=MESH,
        ),
    ]
    downs = [
        pltpu.make_async_remote_copy(
            frames.at[pl.ds(0, EDGE)], halo.at[pl.ds(EDGE, EDGE)],
            send.at[2], recv.at[2], device_id=down, device_id_type=MESH,
        ),
        pltpu.make_async_remote_copy(
            labels.at[pl.ds(0, 8)], lab_high,
            send.at[3], recv.at[3], device_id=down, device_id_type=MESH,
        ),
    ]
    has_low = me > 0
    has_high = me < tm_count - 1
    barrier = pltpu.get_barrier_semaphore()

    @pl.when(has_low)
    def _():
        pl.semaphore_signal(barrier, inc=1, device_id=down, device_id_type=MESH)

    @pl.when(has_high)
    def _():
        pl.semaphore_signal(barrier, inc=1, device_id=up, device_id_type=MESH)

    inner = jnp.logical_and(has_low, has_high)

    @pl.when(inner)
    def _():
        pl.semaphore_wait(barrier, 2)

    @pl.when(jnp.logical_not(inner))
    def _():
        pl.semaphore_wait(barrier, 1)

    @pl.when(has_high)
    def _():
        for copy in ups:
            copy.start()

    @pl.when(has_low)
    def _():
        for copy in downs:
            copy.start()

    @pl.when(jnp.logical_not(has_low))
    def _():
        halo[pl.ds(0, EDGE), :] = jnp.zeros((EDGE, halo.shape[1]), halo.dtype)
        lab_low[...] = jnp.full(lab_low.shape, -1, jnp.int32)

    @pl.when(jnp.logical_not(has_high))
    def _():
        halo[pl.ds(EDGE, EDGE), :] = jnp.zeros((EDGE, halo.shape[1]), halo.dtype)
        lab_high[...] = jnp.full(lab_high.shape, -1, jnp.int32)

    scale = gain[...]
    columns = pl.ds(pl.multiple_of(column * channels, LANES), channels)
    per = CHUNK // LANES
    pooled = jnp.zeros((2 * owned, channels), jnp.float32)

    width = min(channels, 256)
    slices = channels // width
    part = CHUNK // slices

    def prepare(k, j):
        normed[k % 2, pl.ds(j * part, part), :] = normalised(
            held[pl.ds(k * CHUNK + j * part, part), :], scale
        )

    def store(start, size, sem):
        here = pl.ds(start, size)
        return pltpu.make_async_copy(made.at[here], glu_out.at[here], out_sems.at[sem])

    stores = [store(EDGE + k * CHUNK, CHUNK, k) for k in range(chunks - 1)]
    stores.append(store(EDGE + rows - CHUNK, CHUNK + EDGE, chunks - 1))
    stores.append(store(0, EDGE, chunks))

    loads[0].wait()
    for j in range(slices):
        prepare(0, j)
    for copy in weights:
        copy.wait()
    for k in range(chunks):
        size = CHUNK
        if k + 1 < chunks:
            loads[k + 1].wait()
        else:
            size = CHUNK + 2 * EDGE

            @pl.when(has_low)
            def _():
                ups[0].wait_recv()
                ups[1].wait_recv()

            @pl.when(has_high)
            def _():
                downs[0].wait_recv()
                downs[1].wait_recv()

            normed[k % 2, pl.ds(CHUNK, 2 * EDGE), :] = normalised(halo[...], scale)
        block = normed[k % 2, pl.ds(0, size), :]
        for j in range(slices):
            lanes = slice(j * width, (j + 1) * width)
            value = jnp.dot(block, wv[:, lanes], preferred_element_type=jnp.float32)
            gate = jnp.dot(block, wg[:, lanes], preferred_element_type=jnp.float32)
            if k + 1 < chunks:
                prepare(k + 1, j)
            glu = (value * sigmoid(gate)).astype(jnp.bfloat16)
            made[pl.ds(EDGE + k * CHUNK, CHUNK), lanes] = glu[:CHUNK]
            if k == chunks - 1:
                made[pl.ds(0, EDGE), lanes] = glu[CHUNK : CHUNK + EDGE]
                made[pl.ds(EDGE + rows, EDGE), lanes] = glu[CHUNK + EDGE :]
        stores[k].start()
        if k == chunks - 1:
            stores[k + 1].start()
        slots = segs[pl.ds(k * per, per), :] - me * owned
        pooled = pooled + jnp.dot(
            selection(slots, 2 * owned),
            held[pl.ds(k * CHUNK, CHUNK), columns],
            preferred_element_type=jnp.float32,
        )
    pooled_out[...] = pooled
    lab_out[pl.ds(0, 8), :] = lab_low[...]
    lab_out[pl.ds(8, lab_rows), :] = labels[...]
    lab_out[pl.ds(8 + lab_rows, 8), :] = lab_high[...]
    for copy in stores:
        copy.wait()

    @pl.when(has_high)
    def _():
        for copy in ups:
            copy.wait_send()

    @pl.when(has_low)
    def _():
        for copy in downs:
            copy.wait_send()


def conv_kernel(
    glu_hbm, lab_s, lab_v, segs, taps, bn_scale, bn_shift, pooled_hbm, w_hbm,
    message, count_message, own, count_out,
    wide, hidden, lab_wide, w_out, mixed, glu, pooled_frames, sems, glu_sems,
):
    channels = glu.shape[1]
    rows = hidden.shape[0]
    groups = channels // LANES
    kernel = taps.shape[0]
    half = (kernel - 1) // 2
    owned = rows // 32
    me = lax.axis_index("tm")
    column = lax.axis_index("tensor")

    def piece(start, size, k):
        here = pl.ds(start, size)
        return pltpu.make_async_copy(glu_hbm.at[here], glu.at[here], glu_sems.at[k])

    first = piece(0, CHUNK + 2 * EDGE, 0)
    first.start()
    for k in range(1, rows // CHUNK):
        piece(k * CHUNK + 2 * EDGE, CHUNK, k).start()
    late = [
        pltpu.make_async_copy(w_hbm, w_out, sems.at[0]),
        pltpu.make_async_copy(pooled_hbm, pooled_frames, sems.at[1]),
    ]
    for copy in late:
        copy.start()
    first.wait()

    def widen(start, size):
        block = glu[pl.ds(start, size), :].astype(jnp.float32)
        for g in range(groups):
            wide[g, pl.ds(start, size), :] = block[:, g * LANES : (g + 1) * LANES]

    widen(0, 2 * EDGE)

    def finish(acc, start, g, size):
        lanes = slice(g * LANES, (g + 1) * LANES)
        v = acc * bn_scale[:, lanes] + bn_shift[:, lanes]
        hidden[pl.ds(start, size), lanes] = (v * sigmoid(v)).astype(jnp.bfloat16)

    def step(i, carry):
        base = pl.multiple_of(i * LANES, LANES)
        k = i // (CHUNK // LANES)

        @pl.when(jnp.logical_and(i > 0, k * (CHUNK // LANES) == i))
        def _():
            piece(pl.multiple_of(k * CHUNK + 2 * EDGE, 2 * EDGE), CHUNK, k).wait()

        widen(pl.multiple_of(base + 2 * EDGE, 2 * EDGE), LANES)

        def label(at):
            return lab_s[7 + i + (LANES + at) // LANES, (LANES + at) % LANES]

        def plain(o, size):
            for g in range(groups):
                lanes = slice(g * LANES, (g + 1) * LANES)
                acc = jnp.zeros((size, LANES), jnp.float32)
                for t in range(kernel):
                    x = wide[g, pl.ds(base + (o + t + EDGE - half), size), :]
                    acc = acc + taps[t : t + 1, lanes] * x
                finish(acc, base + o, g, size)

        def masked(o, size):
            center = lab_wide[pl.ds(LANES + o, size), :]
            accs = [jnp.zeros((size, LANES), jnp.float32) for _ in range(groups)]
            for t in range(kernel):
                keep = lab_wide[pl.ds(LANES + o + t - half, size), :] == center
                for g in range(groups):
                    lanes = slice(g * LANES, (g + 1) * LANES)
                    x = wide[g, pl.ds(base + (o + t + EDGE - half), size), :]
                    accs[g] = accs[g] + taps[t : t + 1, lanes] * jnp.where(keep, x, 0.0)
            for g in range(groups):
                finish(accs[g], base + o, g, size)

        whole = label(-half) == label(LANES - 1 + half)

        @pl.when(whole)
        def _():
            plain(0, LANES)

        @pl.when(jnp.logical_not(whole))
        def _():
            for d in range(3):
                row = lab_v[pl.ds(7 + i + d, 1), :]
                lab_wide[pl.ds(d * LANES, LANES), :] = jnp.transpose(
                    jnp.broadcast_to(row, (LANES, LANES))
                )
            for o in range(0, LANES, SUB):
                same = label(o - half) == label(o + SUB - 1 + half)
                pl.when(same)(functools.partial(plain, o, SUB))
                pl.when(jnp.logical_not(same))(functools.partial(masked, o, SUB))

        return carry

    lax.fori_loop(0, rows // LANES, step, 0)

    per = CHUNK // LANES
    total = jnp.zeros((2 * owned, channels), jnp.float32)
    tally = jnp.zeros((2 * owned, LANES), jnp.float32)
    for k in range(rows // CHUNK):
        chosen = selection(segs[pl.ds(k * per, per), :] - me * owned, 2 * owned)
        total = total + jnp.dot(
            chosen, hidden[pl.ds(k * CHUNK, CHUNK), :], preferred_element_type=jnp.float32
        )
        wide_chosen = chosen.astype(jnp.float32)
        for q in range(per):
            tally = tally + wide_chosen[:, q * LANES : (q + 1) * LANES]
    count = jnp.broadcast_to(jnp.sum(tally, axis=1, keepdims=True), tally.shape)
    for copy in late:
        copy.wait()
    mixed[...] = jnp.dot(
        total.astype(jnp.bfloat16), w_out[...], preferred_element_type=jnp.float32
    )
    for j in range(message.shape[1]):
        lanes = slice(j * channels, (j + 1) * channels)
        message[0, j] = mixed[:owned, lanes].astype(jnp.bfloat16)
        message[1, j] = mixed[owned:, lanes].astype(jnp.bfloat16)
    columns = pl.ds(pl.multiple_of(column * channels, LANES), channels)
    mine = mixed[:, columns] + pooled_frames[...]
    own[...] = mine[:owned]
    message[1, column] = mine[owned:].astype(jnp.bfloat16)
    count_out[...] = count[:owned]
    count_message[...] = count[owned:].astype(jnp.bfloat16)


def exchange_kernel(
    tm_count, n, message, count_message, own, count_own, out,
    from_peer, from_behind, from_count, send, recv,
):
    me = lax.axis_index("tm")
    column = lax.axis_index("tensor")
    has_low = me > 0
    has_high = me < tm_count - 1
    others = [lax.rem(column + s, n) for s in range(n)]
    barrier = pltpu.get_barrier_semaphore()
    for s in range(1, n):
        pl.semaphore_signal(
            barrier, inc=1, device_id={"tensor": others[s]}, device_id_type=MESH
        )

    @pl.when(has_low)
    def _():
        for s in range(n):
            pl.semaphore_signal(
                barrier, inc=1, device_id=(me - 1, others[s]), device_id_type=MESH
            )

    @pl.when(has_high)
    def _():
        pl.semaphore_wait(barrier, 2 * n - 1)

    @pl.when(jnp.logical_not(has_high))
    def _():
        pl.semaphore_wait(barrier, n - 1)

    ahead = [
        pltpu.make_async_remote_copy(
            message.at[1, others[s]], from_behind.at[s], send.at[s], recv.at[s],
            device_id=(me + 1, others[s]), device_id_type=MESH,
        )
        for s in range(n)
    ] + [
        pltpu.make_async_remote_copy(
            count_message, from_count, send.at[n], recv.at[n],
            device_id=(me + 1, column), device_id_type=MESH,
        )
    ]
    across = [
        pltpu.make_async_remote_copy(
            message.at[0, others[s]], from_peer.at[s], send.at[n + s], recv.at[n + s],
            device_id=(me, others[s]), device_id_type=MESH,
        )
        for s in range(1, n)
    ]

    @pl.when(has_high)
    def _():
        for copy in ahead:
            copy.start()

    for copy in across:
        copy.start()

    @pl.when(jnp.logical_not(has_low))
    def _():
        from_behind[...] = jnp.zeros(from_behind.shape, from_behind.dtype)
        from_count[...] = jnp.zeros(from_count.shape, from_count.dtype)

    for copy in across:
        copy.wait_recv()

    @pl.when(has_low)
    def _():
        for copy in ahead:
            copy.wait_recv()

    total = own[...]
    for s in range(1, n):
        total = total + from_peer[s].astype(jnp.float32)
    for s in range(n):
        total = total + from_behind[s].astype(jnp.float32)
    count = count_own[...] + from_count[...].astype(jnp.float32)
    for g in range(out.shape[1] // LANES):
        lanes = slice(g * LANES, (g + 1) * LANES)
        out[:, lanes] = total[:, lanes] / count
    for copy in across:
        copy.wait_send()

    @pl.when(has_high)
    def _():
        for copy in ahead:
            copy.wait_send()


def shards(
    tm_count, n,
    frames, utt_ids, seg_ids, norm_gain, w_value, w_gate, conv_taps, bn_scale, bn_shift, w_out
):
    rows, width = frames.shape
    channels = w_value.shape[1]
    owned = rows // 32
    lab_rows = rows // LANES
    bf16, f32, i32 = jnp.bfloat16, jnp.float32, jnp.int32
    shape = jax.ShapeDtypeStruct
    dma = pltpu.SemaphoreType.DMA
    labels = utt_ids.reshape(lab_rows, LANES)
    segs = seg_ids.reshape(lab_rows, LANES)
    glu, lab, pooled = pl.pallas_call(
        functools.partial(glu_kernel, tm_count),
        name="glu",
        out_shape=[
            shape((rows + 2 * EDGE, channels), bf16),
            shape((lab_rows + 16, LANES), i32),
            shape((2 * owned, channels), f32),
        ],
        in_specs=[HBM, VMEM, VMEM, VMEM, HBM, HBM],
        out_specs=[HBM, VMEM, VMEM],
        scratch_shapes=[
            pltpu.VMEM((rows, width), bf16),
            pltpu.VMEM((2, CHUNK + 2 * EDGE, width), bf16),
            pltpu.VMEM((2 * EDGE, width), bf16),
            pltpu.VMEM((8, LANES), i32),
            pltpu.VMEM((8, LANES), i32),
            pltpu.VMEM((width, channels), bf16),
            pltpu.VMEM((width, channels), bf16),
            pltpu.VMEM((rows + 2 * EDGE, channels), bf16),
            dma((rows // CHUNK,)),
            dma((2,)),
            dma((4,)),
            dma((4,)),
            dma((rows // CHUNK + 1,)),
        ],
        compiler_params=pltpu.CompilerParams(
            collective_id=0, has_side_effects=True, vmem_limit_bytes=53 * MIB
        ),
    )(frames, labels, segs, norm_gain.reshape(1, width), w_value, w_gate)
    message, count_message, own, count = pl.pallas_call(
        conv_kernel,
        name="conv",
        out_shape=[
            shape((2, n, owned, channels), bf16),
            shape((owned, LANES), bf16),
            shape((owned, channels), f32),
            shape((owned, LANES), f32),
        ],
        in_specs=[HBM, pl.BlockSpec(memory_space=pltpu.SMEM)] + [VMEM] * 5 + [HBM, HBM],
        out_specs=[VMEM] * 4,
        scratch_shapes=[
            pltpu.VMEM((channels // LANES, rows + 2 * EDGE, LANES), f32),
            pltpu.VMEM((rows, channels), bf16),
            pltpu.VMEM((3 * LANES, LANES), i32),
            pltpu.VMEM(w_out.shape, bf16),
            pltpu.VMEM((2 * owned, w_out.shape[1]), f32),
            pltpu.VMEM((rows + 2 * EDGE, channels), bf16),
            pltpu.VMEM((2 * owned, channels), f32),
            dma((2,)),
            dma((rows // CHUNK,)),
        ],
        compiler_params=pltpu.CompilerParams(vmem_limit_bytes=53 * MIB),
    )(
        glu, lab, lab, segs, conv_taps, bn_scale.reshape(1, channels),
        bn_shift.reshape(1, channels), pooled, w_out,
    )
    return pl.pallas_call(
        functools.partial(exchange_kernel, tm_count, n),
        name="exchange",
        out_shape=shape((owned, channels), f32),
        in_specs=[VMEM] * 4,
        out_specs=VMEM,
        scratch_shapes=[
            pltpu.VMEM((n, owned, channels), bf16),
            pltpu.VMEM((n, owned, channels), bf16),
            pltpu.VMEM((owned, LANES), bf16),
            dma((2 * n,)),
            dma((2 * n,)),
        ],
        compiler_params=pltpu.CompilerParams(
            collective_id=1, has_side_effects=True, vmem_limit_bytes=8 * MIB
        ),
    )(message, count_message, own, count)


def solution(mesh):
    in_specs = (
        P("tm", None),
        P("tm"),
        P("tm"),
        P(),
        P(None, "tensor"),
        P(None, "tensor"),
        P(None, "tensor"),
        P("tensor"),
        P("tensor"),
        P("tensor", None),
    )
    out_specs = P("tm", "tensor")
    body = functools.partial(shards, mesh.shape["tm"], mesh.shape["tensor"])
    return jax.shard_map(body, mesh=mesh, in_specs=in_specs, out_specs=out_specs, check_vma=False)
```

```python
import functools

import jax
import jax.numpy as jnp
from jax import lax
from jax.experimental import pallas as pl
from jax.experimental.pallas import tpu as pltpu
from jax.sharding import PartitionSpec as P

MESH = pl.DeviceIdType.MESH
VMEM = pl.BlockSpec(memory_space=pltpu.VMEM)
HBM = pl.BlockSpec(memory_space=pltpu.HBM)
EDGE = 16
LANES = 128
CHUNK = 256
SUB = 64
MIB = 1 << 20


def sigmoid(v):
    return 0.5 + 0.5 * jnp.tanh(0.5 * v)


def normalised(block, gain):
    floats = block.astype(jnp.float32)
    center = jnp.mean(floats, axis=1, keepdims=True)
    moved = floats - center
    spread = jnp.mean(moved * moved, axis=1, keepdims=True)
    return (moved * lax.rsqrt(spread + 1e-05) * gain).astype(jnp.bfloat16)


def selection(slots, slot_count):
    kinds = lax.broadcasted_iota(jnp.int32, (slot_count, LANES), 0)
    rows = [
        jnp.where(kinds == slots[r : r + 1, :], 1.0, 0.0).astype(jnp.bfloat16)
        for r in range(slots.shape[0])
    ]
    return jnp.concatenate(rows, axis=1)


def glu_kernel(
    tm_count, frames, labels, segs, gain, wv_hbm, wg_hbm,
    glu_out, lab_out, pooled_out,
    held, normed, halo, lab_low, lab_high, wv, wg, made, chunk_sems, w_sems, send, recv, out_sems,
):
    rows = frames.shape[0]
    channels = wv.shape[1]
    chunks = rows // CHUNK
    lab_rows = labels.shape[0]
    owned = rows // 32
    me = lax.axis_index("tm")
    column = lax.axis_index("tensor")
    loads = [
        pltpu.make_async_copy(
            frames.at[pl.ds(k * CHUNK, CHUNK)], held.at[pl.ds(k * CHUNK, CHUNK)], chunk_sems.at[k]
        )
        for k in range(chunks)
    ]
    weights = [
        pltpu.make_async_copy(wv_hbm, wv, w_sems.at[0]),
        pltpu.make_async_copy(wg_hbm, wg, w_sems.at[1]),
    ]
    loads[0].start()
    for copy in weights + loads[1:]:
        copy.start()
    up = {"tm": me + 1}
    down = {"tm": me - 1}
    ups = [
        pltpu.make_async_remote_copy(
            frames.at[pl.ds(rows - EDGE, EDGE)], halo.at[pl.ds(0, EDGE)],
            send.at[0], recv.at[0], device_id=up, device_id_type=MESH,
        ),
        pltpu.make_async_remote_copy(
            labels.at[pl.ds(lab_rows - 8, 8)], lab_low,
            send.at[1], recv.at[1], device_id=up, device_id_type=MESH,
        ),
    ]
    downs = [
        pltpu.make_async_remote_copy(
            frames.at[pl.ds(0, EDGE)], halo.at[pl.ds(EDGE, EDGE)],
            send.at[2], recv.at[2], device_id=down, device_id_type=MESH,
        ),
        pltpu.make_async_remote_copy(
            labels.at[pl.ds(0, 8)], lab_high,
            send.at[3], recv.at[3], device_id=down, device_id_type=MESH,
        ),
    ]
    has_low = me > 0
    has_high = me < tm_count - 1
    barrier = pltpu.get_barrier_semaphore()

    @pl.when(has_low)
    def _():
        pl.semaphore_signal(barrier, inc=1, device_id=down, device_id_type=MESH)

    @pl.when(has_high)
    def _():
        pl.semaphore_signal(barrier, inc=1, device_id=up, device_id_type=MESH)

    inner = jnp.logical_and(has_low, has_high)

    @pl.when(inner)
    def _():
        pl.semaphore_wait(barrier, 2)

    @pl.when(jnp.logical_not(inner))
    def _():
        pl.semaphore_wait(barrier, 1)

    @pl.when(has_high)
    def _():
        for copy in ups:
            copy.start()

    @pl.when(has_low)
    def _():
        for copy in downs:
            copy.start()

    @pl.when(jnp.logical_not(has_low))
    def _():
        halo[pl.ds(0, EDGE), :] = jnp.zeros((EDGE, halo.shape[1]), halo.dtype)
        lab_low[...] = jnp.full(lab_low.shape, -1, jnp.int32)

    @pl.when(jnp.logical_not(has_high))
    def _():
        halo[pl.ds(EDGE, EDGE), :] = jnp.zeros((EDGE, halo.shape[1]), halo.dtype)
        lab_high[...] = jnp.full(lab_high.shape, -1, jnp.int32)

    scale = gain[...]
    columns = pl.ds(pl.multiple_of(column * channels, LANES), channels)
    per = CHUNK // LANES
    pooled = jnp.zeros((2 * owned, channels), jnp.float32)

    width = min(channels, 256)
    slices = channels // width
    part = CHUNK // slices

    def prepare(k, j):
        normed[k % 2, pl.ds(j * part, part), :] = normalised(
            held[pl.ds(k * CHUNK + j * part, part), :], scale
        )

    def store(start, size, sem):
        here = pl.ds(start, size)
        return pltpu.make_async_copy(made.at[here], glu_out.at[here], out_sems.at[sem])

    stores = [store(EDGE + k * CHUNK, CHUNK, k) for k in range(chunks - 1)]
    stores.append(store(EDGE + rows - CHUNK, CHUNK + EDGE, chunks - 1))
    stores.append(store(0, EDGE, chunks))

    loads[0].wait()
    for j in range(slices):
        prepare(0, j)
    for copy in weights:
        copy.wait()
    for k in range(chunks):
        size = CHUNK
        if k + 1 < chunks:
            loads[k + 1].wait()
        else:
            size = CHUNK + 2 * EDGE

            @pl.when(has_low)
            def _():
                ups[0].wait_recv()
                ups[1].wait_recv()

            @pl.when(has_high)
            def _():
                downs[0].wait_recv()
                downs[1].wait_recv()

            normed[k % 2, pl.ds(CHUNK, 2 * EDGE), :] = normalised(halo[...], scale)
        block = normed[k % 2, pl.ds(0, size), :]
        for j in range(slices):
            lanes = slice(j * width, (j + 1) * width)
            value = jnp.dot(block, wv[:, lanes], preferred_element_type=jnp.float32)
            gate = jnp.dot(block, wg[:, lanes], preferred_element_type=jnp.float32)
            if k + 1 < chunks:
                prepare(k + 1, j)
            glu = (value * sigmoid(gate)).astype(jnp.bfloat16)
            made[pl.ds(EDGE + k * CHUNK, CHUNK), lanes] = glu[:CHUNK]
            if k == chunks - 1:
                made[pl.ds(0, EDGE), lanes] = glu[CHUNK : CHUNK + EDGE]
                made[pl.ds(EDGE + rows, EDGE), lanes] = glu[CHUNK + EDGE :]
        stores[k].start()
        if k == chunks - 1:
            stores[k + 1].start()
        slots = segs[pl.ds(k * per, per), :] - me * owned
        pooled = pooled + jnp.dot(
            selection(slots, 2 * owned),
            held[pl.ds(k * CHUNK, CHUNK), columns],
            preferred_element_type=jnp.float32,
        )
    pooled_out[...] = pooled
    lab_out[pl.ds(0, 8), :] = lab_low[...]
    lab_out[pl.ds(8, lab_rows), :] = labels[...]
    lab_out[pl.ds(8 + lab_rows, 8), :] = lab_high[...]
    for copy in stores:
        copy.wait()

    @pl.when(has_high)
    def _():
        for copy in ups:
            copy.wait_send()

    @pl.when(has_low)
    def _():
        for copy in downs:
            copy.wait_send()


def conv_kernel(
    glu_hbm, lab_s, lab_v, segs, taps, bn_scale, bn_shift, pooled_hbm, w_hbm,
    message, count_message, own, count_out,
    wide, hidden, lab_wide, w_out, mixed, glu, pooled_frames, sems, glu_sems,
):
    channels = glu.shape[1]
    rows = hidden.shape[0]
    groups = channels // LANES
    kernel = taps.shape[0]
    half = (kernel - 1) // 2
    owned = rows // 32
    me = lax.axis_index("tm")
    column = lax.axis_index("tensor")

    def piece(start, size, k):
        here = pl.ds(start, size)
        return pltpu.make_async_copy(glu_hbm.at[here], glu.at[here], glu_sems.at[k])

    first = piece(0, CHUNK + 2 * EDGE, 0)
    first.start()
    for k in range(1, rows // CHUNK):
        piece(k * CHUNK + 2 * EDGE, CHUNK, k).start()
    late = [
        pltpu.make_async_copy(w_hbm, w_out, sems.at[0]),
        pltpu.make_async_copy(pooled_hbm, pooled_frames, sems.at[1]),
    ]
    for copy in late:
        copy.start()
    first.wait()

    def widen(start, size):
        block = glu[pl.ds(start, size), :].astype(jnp.float32)
        for g in range(groups):
            wide[g, pl.ds(start, size), :] = block[:, g * LANES : (g + 1) * LANES]

    widen(0, 2 * EDGE)

    def finish(acc, start, g, size):
        lanes = slice(g * LANES, (g + 1) * LANES)
        v = acc * bn_scale[:, lanes] + bn_shift[:, lanes]
        hidden[pl.ds(start, size), lanes] = (v * sigmoid(v)).astype(jnp.bfloat16)

    def step(i, carry):
        base = pl.multiple_of(i * LANES, LANES)
        k = i // (CHUNK // LANES)

        @pl.when(jnp.logical_and(i > 0, k * (CHUNK // LANES) == i))
        def _():
            piece(pl.multiple_of(k * CHUNK + 2 * EDGE, 2 * EDGE), CHUNK, k).wait()

        widen(pl.multiple_of(base + 2 * EDGE, 2 * EDGE), LANES)

        def label(at):
            return lab_s[7 + i + (LANES + at) // LANES, (LANES + at) % LANES]

        def plain(o, size):
            for g in range(groups):
                lanes = slice(g * LANES, (g + 1) * LANES)
                acc = jnp.zeros((size, LANES), jnp.float32)
                for t in range(kernel):
                    x = wide[g, pl.ds(base + (o + t + EDGE - half), size), :]
                    acc = acc + taps[t : t + 1, lanes] * x
                finish(acc, base + o, g, size)

        def masked(o, size):
            center = lab_wide[pl.ds(LANES + o, size), :]
            accs = [jnp.zeros((size, LANES), jnp.float32) for _ in range(groups)]
            for t in range(kernel):
                keep = lab_wide[pl.ds(LANES + o + t - half, size), :] == center
                for g in range(groups):
                    lanes = slice(g * LANES, (g + 1) * LANES)
                    x = wide[g, pl.ds(base + (o + t + EDGE - half), size), :]
                    accs[g] = accs[g] + taps[t : t + 1, lanes] * jnp.where(keep, x, 0.0)
            for g in range(groups):
                finish(accs[g], base + o, g, size)

        whole = label(-half) == label(LANES - 1 + half)

        @pl.when(whole)
        def _():
            plain(0, LANES)

        @pl.when(jnp.logical_not(whole))
        def _():
            for d in range(3):
                row = lab_v[pl.ds(7 + i + d, 1), :]
                lab_wide[pl.ds(d * LANES, LANES), :] = jnp.transpose(
                    jnp.broadcast_to(row, (LANES, LANES))
                )
            for o in range(0, LANES, SUB):
                same = label(o - half) == label(o + SUB - 1 + half)
                pl.when(same)(functools.partial(plain, o, SUB))
                pl.when(jnp.logical_not(same))(functools.partial(masked, o, SUB))

        return carry

    lax.fori_loop(0, rows // LANES, step, 0)

    per = CHUNK // LANES
    total = jnp.zeros((2 * owned, channels), jnp.float32)
    tally = jnp.zeros((2 * owned, LANES), jnp.float32)
    for k in range(rows // CHUNK):
        chosen = selection(segs[pl.ds(k * per, per), :] - me * owned, 2 * owned)
        total = total + jnp.dot(
            chosen, hidden[pl.ds(k * CHUNK, CHUNK), :], preferred_element_type=jnp.float32
        )
        wide_chosen = chosen.astype(jnp.float32)
        for q in range(per):
            tally = tally + wide_chosen[:, q * LANES : (q + 1) * LANES]
    count = jnp.broadcast_to(jnp.sum(tally, axis=1, keepdims=True), tally.shape)
    for copy in late:
        copy.wait()
    mixed[...] = jnp.dot(
        total.astype(jnp.bfloat16), w_out[...], preferred_element_type=jnp.float32
    )
    for j in range(message.shape[1]):
        lanes = slice(j * channels, (j + 1) * channels)
        message[0, j] = mixed[:owned, lanes].astype(jnp.bfloat16)
        message[1, j] = mixed[owned:, lanes].astype(jnp.bfloat16)
    columns = pl.ds(pl.multiple_of(column * channels, LANES), channels)
    mine = mixed[:, columns] + pooled_frames[...]
    own[...] = mine[:owned]
    message[1, column] = mine[owned:].astype(jnp.bfloat16)
    count_out[...] = count[:owned]
    count_message[...] = count[owned:].astype(jnp.bfloat16)


def exchange_kernel(
    tm_count, n, message, count_message, own, count_own, out,
    from_peer, from_behind, from_count, send, recv,
):
    me = lax.axis_index("tm")
    column = lax.axis_index("tensor")
    has_low = me > 0
    has_high = me < tm_count - 1
    others = [lax.rem(column + s, n) for s in range(n)]
    barrier = pltpu.get_barrier_semaphore()
    for s in range(1, n):
        pl.semaphore_signal(
            barrier, inc=1, device_id={"tensor": others[s]}, device_id_type=MESH
        )

    @pl.when(has_low)
    def _():
        for s in range(n):
            pl.semaphore_signal(
                barrier, inc=1, device_id=(me - 1, others[s]), device_id_type=MESH
            )

    @pl.when(has_high)
    def _():
        pl.semaphore_wait(barrier, 2 * n - 1)

    @pl.when(jnp.logical_not(has_high))
    def _():
        pl.semaphore_wait(barrier, n - 1)

    ahead = [
        pltpu.make_async_remote_copy(
            message.at[1, others[s]], from_behind.at[s], send.at[s], recv.at[s],
            device_id=(me + 1, others[s]), device_id_type=MESH,
        )
        for s in range(n)
    ] + [
        pltpu.make_async_remote_copy(
            count_message, from_count, send.at[n], recv.at[n],
            device_id=(me + 1, column), device_id_type=MESH,
        )
    ]
    across = [
        pltpu.make_async_remote_copy(
            message.at[0, others[s]], from_peer.at[s], send.at[n + s], recv.at[n + s],
            device_id=(me, others[s]), device_id_type=MESH,
        )
        for s in range(1, n)
    ]

    @pl.when(has_high)
    def _():
        for copy in ahead:
            copy.start()

    for copy in across:
        copy.start()

    @pl.when(jnp.logical_not(has_low))
    def _():
        from_behind[...] = jnp.zeros(from_behind.shape, from_behind.dtype)
        from_count[...] = jnp.zeros(from_count.shape, from_count.dtype)

    for copy in across:
        copy.wait_recv()

    @pl.when(has_low)
    def _():
        for copy in ahead:
            copy.wait_recv()

    total = own[...]
    for s in range(1, n):
        total = total + from_peer[s].astype(jnp.float32)
    for s in range(n):
        total = total + from_behind[s].astype(jnp.float32)
    count = count_own[...] + from_count[...].astype(jnp.float32)
    for g in range(out.shape[1] // LANES):
        lanes = slice(g * LANES, (g + 1) * LANES)
        out[:, lanes] = total[:, lanes] / count
    for copy in across:
        copy.wait_send()

    @pl.when(has_high)
    def _():
        for copy in ahead:
            copy.wait_send()


def shards(
    tm_count, n,
    frames, utt_ids, seg_ids, norm_gain, w_value, w_gate, conv_taps, bn_scale, bn_shift, w_out
):
    rows, width = frames.shape
    channels = w_value.shape[1]
    owned = rows // 32
    lab_rows = rows // LANES
    bf16, f32, i32 = jnp.bfloat16, jnp.float32, jnp.int32
    shape = jax.ShapeDtypeStruct
    dma = pltpu.SemaphoreType.DMA
    labels = utt_ids.reshape(lab_rows, LANES)
    segs = seg_ids.reshape(lab_rows, LANES)
    glu, lab, pooled = pl.pallas_call(
        functools.partial(glu_kernel, tm_count),
        name="glu",
        out_shape=[
            shape((rows + 2 * EDGE, channels), bf16),
            shape((lab_rows + 16, LANES), i32),
            shape((2 * owned, channels), f32),
        ],
        in_specs=[HBM, VMEM, VMEM, VMEM, HBM, HBM],
        out_specs=[HBM, VMEM, VMEM],
        scratch_shapes=[
            pltpu.VMEM((rows, width), bf16),
            pltpu.VMEM((2, CHUNK + 2 * EDGE, width), bf16),
            pltpu.VMEM((2 * EDGE, width), bf16),
            pltpu.VMEM((8, LANES), i32),
            pltpu.VMEM((8, LANES), i32),
            pltpu.VMEM((width, channels), bf16),
            pltpu.VMEM((width, channels), bf16),
            pltpu.VMEM((rows + 2 * EDGE, channels), bf16),
            dma((rows // CHUNK,)),
            dma((2,)),
            dma((4,)),
            dma((4,)),
            dma((rows // CHUNK + 1,)),
        ],
        compiler_params=pltpu.CompilerParams(
            collective_id=0, has_side_effects=True, vmem_limit_bytes=54 * MIB
        ),
    )(frames, labels, segs, norm_gain.reshape(1, width), w_value, w_gate)
    message, count_message, own, count = pl.pallas_call(
        conv_kernel,
        name="conv",
        out_shape=[
            shape((2, n, owned, channels), bf16),
            shape((owned, LANES), bf16),
            shape((owned, channels), f32),
            shape((owned, LANES), f32),
        ],
        in_specs=[HBM, pl.BlockSpec(memory_space=pltpu.SMEM)] + [VMEM] * 5 + [HBM, HBM],
        out_specs=[VMEM] * 4,
        scratch_shapes=[
            pltpu.VMEM((channels // LANES, rows + 2 * EDGE, LANES), f32),
            pltpu.VMEM((rows, channels), bf16),
            pltpu.VMEM((3 * LANES, LANES), i32),
            pltpu.VMEM(w_out.shape, bf16),
            pltpu.VMEM((2 * owned, w_out.shape[1]), f32),
            pltpu.VMEM((rows + 2 * EDGE, channels), bf16),
            pltpu.VMEM((2 * owned, channels), f32),
            dma((2,)),
            dma((rows // CHUNK,)),
        ],
        compiler_params=pltpu.CompilerParams(vmem_limit_bytes=53 * MIB),
    )(
        glu, lab, lab, segs, conv_taps, bn_scale.reshape(1, channels),
        bn_shift.reshape(1, channels), pooled, w_out,
    )
    return pl.pallas_call(
        functools.partial(exchange_kernel, tm_count, n),
        name="exchange",
        out_shape=shape((owned, channels), f32),
        in_specs=[VMEM] * 4,
        out_specs=VMEM,
        scratch_shapes=[
            pltpu.VMEM((n, owned, channels), bf16),
            pltpu.VMEM((n, owned, channels), bf16),
            pltpu.VMEM((owned, LANES), bf16),
            dma((2 * n,)),
            dma((2 * n,)),
        ],
        compiler_params=pltpu.CompilerParams(
            collective_id=1, has_side_effects=True, vmem_limit_bytes=8 * MIB
        ),
    )(message, count_message, own, count)


def solution(mesh):
    in_specs = (
        P("tm", None),
        P("tm"),
        P("tm"),
        P(),
        P(None, "tensor"),
        P(None, "tensor"),
        P(None, "tensor"),
        P("tensor"),
        P("tensor"),
        P("tensor", None),
    )
    out_specs = P("tm", "tensor")
    body = functools.partial(shards, mesh.shape["tm"], mesh.shape["tensor"])
    return jax.shard_map(body, mesh=mesh, in_specs=in_specs, out_specs=out_specs, check_vma=False)
```
